32 devices in a mesh: expert: 8 (over y, x, core), token: 4 (over z).
Axes of the slice: x: 2, y: 2, z: 4, core: 2. Of those that a mesh axis runs over, the one named last changes fastest.
Arguments:
- activations: bfloat16 [16, 1024, 768], P('expert', 'token'), may hold values from -6 to 6
- routed: int32 [16, 1024], P('expert', 'token'), may hold values 0 or 1
- weights: bfloat16 [128, 768, 256], P(('expert', 'token')), may hold values from -6 to 6, as said below
- kept_mask: int32 [128, 768, 256], P(('expert', 'token')), may hold values 0 or 1
- step_counts: int32 [128], P(('expert', 'token')), may hold values from 1 to 7
- ridge_scale: float32 [128], P(('expert', 'token')), may hold values from 0.05 to 0.5
Outputs:
- rebuilt: float32 [128, 768, 256], P(('expert', 'token'))
- misfit: float32 [16], P('expert')
The draws below stay inside these ranges and needn't reach their ends.
Inputs may be any that keep to these rules, and one draw needn't show every extreme that they name: `weights`: every entry's magnitude is at least 0.25.
All inputs are finite; a program needn't handle non-finite values. No bound on the sum of `routed` or of `kept_mask` on one device may be relied on, other than what follows from the above.
Results may differ from the reference program's by a relative error of at most 0.0003.
Values may be sent and summed in bfloat16 or wider, within the bound.
A program may use at most 64 MiB of HBM per device.

```python
import math
import jax
import jax.numpy as jnp
from jax import lax

FF = 768
D = 2048
COLS = 256
EXPERTS = 16
CAL = 1024
TASKS = 128


def draw_weights(key, part):
    base = jnp.clip(jax.random.normal(key, (TASKS, FF, COLS), jnp.float32), -5.75, 5.75)
    return (base + jnp.where(base >= 0.0, 0.25, -0.25)).astype(jnp.bfloat16)


def touch_ends(entries, stream_key, low, largest):
    index_at = [jax.random.randint(jax.random.fold_in(stream_key, axis), (), 0, length) for axis, length in enumerate(entries.shape)]
    main_axis = entries.shape.index(max(entries.shape))
    next_to = index_at[:main_axis] + [(index_at[main_axis] + 1) % entries.shape[main_axis]] + index_at[main_axis + 1:]
    return entries.at[tuple(index_at)].set(low).at[tuple(next_to)].set(largest)


def shard_levels(rng, shape, split, low, top_value):
    def one(axis_at, blocks):
        draws = jax.random.uniform(jax.random.fold_in(jax.random.fold_in(rng, 6), axis_at), (blocks,), jnp.float32, low / len(split), top_value / len(split))
        return jnp.repeat(jnp.exp(draws), shape[axis_at] // blocks).reshape((-1,) + (1,) * (len(shape) - axis_at - 1))

    level = one(*split[0])
    for cut in split[1:]:
        level = level * one(*cut)
    return level


def scatter_about(rng, shape, deviation, limit, shards=(), kind=jnp.bfloat16):
    values = jax.random.normal(rng, shape, jnp.float32) * deviation
    if len(shards) > 0:
        values = shard_levels(rng, shape, shards, -0.22, 0.18) * values
    return jnp.clip(values, min=-limit, max=limit).astype(kind)


def setup_inputs(seed: int = 0) -> dict:
    seeds = jax.random.split(jax.random.key(seed), 7)
    activations = scatter_about(seeds[0], (EXPERTS, CAL, FF), 1.0, 6.0, ((0, 8), (1, 4)))
    routed = touch_ends((jax.random.randint(seeds[1], (EXPERTS, CAL), 0, 4) < 3).astype(jnp.int32), jax.random.fold_in(seeds[1], 1), 0, 1)
    weights = draw_weights(jax.random.fold_in(seeds[6], 71), 0)
    kept_mask = touch_ends((jax.random.randint(seeds[3], (TASKS, FF, COLS), 0, 2) < 1).astype(jnp.int32), jax.random.fold_in(seeds[3], 1), 0, 1)
    step_counts = touch_ends(jax.random.randint(seeds[4], (TASKS,), 1, 8), jax.random.fold_in(seeds[4], 1), 1, 7).astype(jnp.int32)
    ridge_scale = jnp.clip(jnp.exp(math.log(0.5) - 2.3025851 * jax.random.uniform(seeds[5], (TASKS,), jnp.float32) ** shard_levels(seeds[5], (TASKS,), ((0, 32),), -0.2, 0.2)), 0.05, 0.5)
    return dict(activations=activations, routed=routed, weights=weights, kept_mask=kept_mask, step_counts=step_counts, ridge_scale=ridge_scale)


def solve_task(gram_matrix, frobenius, task_weights, task_mask, task_count, task_ridge):
    float_weights = task_weights.astype(jnp.float32)
    float_mask = task_mask.astype(jnp.float32)
    damping = task_ridge * frobenius
    step_size = 1.0 / (frobenius + damping)

    def advance(turn_index, current):
        gradient = jnp.dot(gram_matrix, current - float_weights, precision=lax.Precision.HIGHEST) + damping * current
        return current - step_size * (float_mask * gradient)
    result = lax.fori_loop(0, task_count, advance, float_mask * float_weights)
    change = result - float_weights
    numerator = jnp.sum(change * jnp.dot(gram_matrix, change, precision=lax.Precision.HIGHEST))
    energy = jnp.sum(float_weights * jnp.dot(gram_matrix, float_weights, precision=lax.Precision.HIGHEST))
    return (result, numerator, energy)

def reference(activations, routed, weights, kept_mask, step_counts, ridge_scale):
    per_expert = D // COLS

    def one_expert(packed):
        expert_acts, expert_routed, group_weights, group_mask, group_counts, group_ridge = packed
        masked = expert_acts * expert_routed[:, None].astype(jnp.bfloat16)
        gram_matrix = lax.dot_general(masked, masked, (((0,), (0,)), ((), ())), preferred_element_type=jnp.float32) / CAL
        frobenius = jnp.sqrt(jnp.sum(gram_matrix * gram_matrix))

        def one_task(task_args):
            task_weights, task_mask, task_count, task_ridge = task_args
            return solve_task(gram_matrix, frobenius, task_weights, task_mask, task_count, task_ridge)
        rebuilt_group, numerators, energies = lax.map(one_task, (group_weights, group_mask, group_counts, group_ridge))
        return (rebuilt_group, jnp.sum(numerators), jnp.sum(energies))
    grouped = (activations, routed, weights.reshape(EXPERTS, per_expert, FF, COLS), kept_mask.reshape(EXPERTS, per_expert, FF, COLS), step_counts.reshape(EXPERTS, per_expert), ridge_scale.reshape(EXPERTS, per_expert))
    rebuilt, expert_numer, expert_energy = lax.map(one_expert, grouped)
    misfit = expert_numer / (jnp.sum(expert_energy) / EXPERTS + 1e-06)
    return (rebuilt.reshape(TASKS, FF, COLS), misfit)
```

```python
import functools

import jax
import jax.numpy as jnp
from jax import lax
from jax.experimental import pallas as pl
from jax.experimental.pallas import tpu as pltpu
from jax.sharding import PartitionSpec as P

D = 2048
COLS = 256
MESH = pl.DeviceIdType.MESH
PASSES = 3


def dot(a, b):
    return jnp.dot(a, b, preferred_element_type=jnp.float32)


def split(value):
    high = value.astype(jnp.bfloat16)
    return high, (value - high.astype(jnp.float32)).astype(jnp.bfloat16)


def gram_kernel(
    tokens, group, x_ref, w_hbm, high_ref, low_ref, stats_ref,
    recv, total, outer, w_buf, w_sem, send_sem, recv_sem,
):
    slots, rows, features = x_ref.shape
    block = features // 3 if features % 384 == 0 else features
    me = lax.axis_index("token")
    own = me // group
    load = pltpu.make_async_copy(w_hbm, w_buf, w_sem)
    load.start()

    has_left = me > 0
    has_right = me < tokens - 1
    barrier = pltpu.get_barrier_semaphore()

    @pl.when(has_left)
    def _():
        pl.semaphore_signal(barrier, inc=1, device_id={"token": me - 1}, device_id_type=MESH)

    @pl.when(has_right)
    def _():
        pl.semaphore_signal(barrier, inc=1, device_id={"token": me + 1}, device_id_type=MESH)

    pl.semaphore_wait(barrier, has_left.astype(jnp.int32) + has_right.astype(jnp.int32))

    def sends(way, k, slot):
        if way == 0:
            return has_right & (me - k >= 0) & ((slot + 1) * group - 1 >= me + 1)
        return has_left & (me + k < tokens) & (slot * group <= me - 1)

    def receives(way, k, slot):
        if way == 0:
            return (me - 1 - k >= 0) & ((slot + 1) * group - 1 >= me)
        return (me + 1 + k < tokens) & (slot * group <= me)

    def copy(way, k, slot, source, origin):
        return pltpu.make_async_remote_copy(
            src_ref=source,
            dst_ref=recv.at[slot, origin],
            send_sem=send_sem.at[way, k, slot],
            recv_sem=recv_sem.at[way, k, slot],
            device_id={"token": me + 1 if way == 0 else me - 1},
            device_id_type=MESH,
        )

    def slot_order(way):
        return range(slots - 1, -1, -1) if way == 0 else range(slots)

    def add_gram(rows_ref):
        value = rows_ref[...]
        for start in range(0, features, block):
            total[start : start + block, :] += lax.dot_general(
                value[:, start : start + block], value, (((0,), (0,)), ((), ())),
                preferred_element_type=jnp.float32,
            )

    for place in range(slots):
        for way in range(2):
            slot = list(slot_order(way))[place]

            @pl.when(sends(way, 0, slot))
            def _(way=way, slot=slot):
                copy(way, 0, slot, x_ref.at[slot], me).start()

    total[...] = jnp.zeros_like(total)
    add_gram(x_ref.at[own])
    outer[...] = jnp.zeros_like(outer)
    load.wait()

    @pl.loop(0, w_buf.shape[0])
    def _(task):
        value = w_buf[task]
        for start in range(0, features, block):
            outer[start : start + block, :] += lax.dot_general(
                value[start : start + block, :], value, (((1,), (1,)), ((), ())),
                preferred_element_type=jnp.float32,
            )

    def origin_of(way, k):
        return me - 1 - k if way == 0 else me + 1 + k

    @pl.loop(0, tokens - 1)
    def _(k):
        for place in range(slots):
            for way in range(2):
                slot = list(slot_order(way))[place]
                origin = origin_of(way, k)

                @pl.when(sends(way, k + 1, slot))
                def _(way=way, slot=slot, origin=origin):
                    copy(way, k, slot, x_ref.at[slot], origin).wait_recv()
                    copy(way, k + 1, slot, recv.at[slot, origin], origin).start()

        for way in range(2):

            @pl.when(sends(way, k + 1, own))
            def _(way=way):
                add_gram(recv.at[own, origin_of(way, k)])

    @pl.loop(0, tokens - 1)
    def _(k):
        for way in range(2):

            @pl.when(receives(way, k, own) & jnp.logical_not(sends(way, k + 1, own)))
            def _(way=way):
                origin = origin_of(way, k)
                copy(way, k, own, x_ref.at[own], origin).wait_recv()
                add_gram(recv.at[own, origin])

    scale = 1.0 / (rows * tokens)
    square = jnp.zeros((1, features), jnp.float32)
    energy = jnp.zeros((1, features), jnp.float32)
    piece = block // 4
    for start in range(0, features, piece):
        part = total[start : start + piece, :] * scale
        high, low = split(part)
        high_ref[start : start + piece, :] = high
        low_ref[start : start + piece, :] = low
        square = square + jnp.sum(part * part, axis=0, keepdims=True)
        energy = energy + jnp.sum(part * outer[start : start + piece, :], axis=0, keepdims=True)
    stats_ref[0] = jnp.sum(square)
    stats_ref[1] = jnp.sum(energy)

    @pl.loop(0, tokens - 1)
    def _(k):
        for way in range(2):
            for slot in range(slots):

                @pl.when(sends(way, k, slot))
                def _(way=way, slot=slot):
                    copy(way, k, slot, x_ref.at[slot], me).wait_send()


def gram_call(tokens, group, masked, weights):
    slots, rows, features = masked.shape
    vmem = pl.BlockSpec(memory_space=pltpu.VMEM)
    hops = max(tokens, 2)
    return pl.pallas_call(
        functools.partial(gram_kernel, tokens, group),
        out_shape=(
            jax.ShapeDtypeStruct((features, features), jnp.bfloat16),
            jax.ShapeDtypeStruct((features, features), jnp.bfloat16),
            jax.ShapeDtypeStruct((2,), jnp.float32),
        ),
        in_specs=[vmem, pl.BlockSpec(memory_space=pl.ANY)],
        out_specs=(vmem, vmem, pl.BlockSpec(memory_space=pltpu.SMEM)),
        scratch_shapes=[
            pltpu.VMEM((slots, tokens, rows, features), jnp.bfloat16),
            pltpu.VMEM((features, features), jnp.float32),
            pltpu.VMEM((features, features), jnp.float32),
            pltpu.VMEM(weights.shape, weights.dtype),
            pltpu.SemaphoreType.DMA,
            pltpu.SemaphoreType.DMA((2, hops, slots)),
            pltpu.SemaphoreType.DMA((2, hops, slots)),
        ],
        compiler_params=pltpu.CompilerParams(
            collective_id=0, has_side_effects=True, vmem_limit_bytes=48 << 20
        ),
    )(masked, weights)


def solve_kernel(
    group, counts_ref, ridge_ref, stats_ref, high_ref, low_ref, w_ref, mask_ref,
    out_ref, payload_ref, delta, first, cross, scaled_mask, turn_ref,
):
    task = pl.program_id(0)
    features, columns = delta.shape
    block = features // 3 if features % 384 == 0 else features
    starts = range(0, features, block)
    row = (1, columns)
    frobenius = jnp.sqrt(jnp.full(row, stats_ref[0], jnp.float32))
    damping = ridge_ref[task] * frobenius
    step = 1.0 / (frobenius + damping)
    shrink = step * damping

    def times_gram(start, right_high, right_low):
        top = high_ref[start : start + block, :]
        result = dot(top, right_high)
        if PASSES >= 2:
            result += dot(low_ref[start : start + block, :], right_high)
        if PASSES >= 3:
            result += dot(top, right_low)
        return result

    pruned = jnp.where(mask_ref[0] == 0, w_ref[0], jnp.zeros_like(w_ref[0]))
    for start in starts:
        at = slice(start, start + block)
        kept = mask_ref[0, at, :].astype(jnp.float32)
        product = dot(high_ref[at, :], pruned) + dot(low_ref[at, :], pruned)
        cross[at, :] = product
        begin = kept * (step * product - shrink * w_ref[0, at, :].astype(jnp.float32))
        first[at, :] = begin
        delta[at, :] = begin
        scaled_mask[at, :] = kept * step

    @pl.loop(1, counts_ref[task])
    def _(turn):
        right_high, right_low = split(delta[...])
        for start in starts:
            at = slice(start, start + block)
            product = times_gram(start, right_high, right_low)
            delta[at, :] = (
                (1.0 - shrink) * delta[at, :] + first[at, :] - scaled_mask[at, :] * product
            )

    right_high, right_low = split(delta[...])
    numerator = jnp.zeros(row, jnp.float32)
    for start in starts:
        at = slice(start, start + block)
        product = times_gram(start, right_high, right_low)
        weight = w_ref[0, at, :].astype(jnp.float32)
        kept = mask_ref[0, at, :] != 0
        value = delta[at, :] + jnp.where(kept, weight, 0.0)
        out_ref[0, at, :] = value
        numerator = numerator + jnp.sum(
            (value - weight) * (product - cross[at, :]), axis=0, keepdims=True
        )

    own = lax.axis_index("token") // group
    lanes = lax.broadcasted_iota(jnp.int32, payload_ref.shape, 1)
    lines = lax.broadcasted_iota(jnp.int32, payload_ref.shape, 0)

    @pl.when(task == 0)
    def _():
        payload_ref[...] = jnp.where(lines == 0, stats_ref[1], 0.0)

    payload_ref[...] += jnp.where((lines == 1) & (lanes == own), jnp.sum(numerator), 0.0)


def solve_call(group, counts, ridge, stats, high, low, weights, mask):
    tasks, features, columns = weights.shape
    smem = pl.BlockSpec(memory_space=pltpu.SMEM)
    vmem = pl.BlockSpec(memory_space=pltpu.VMEM)
    item = pl.BlockSpec((1, features, columns), lambda i: (i, 0, 0))
    plane = pltpu.VMEM((features, columns), jnp.float32)
    return pl.pallas_call(
        functools.partial(solve_kernel, group),
        grid=(tasks,),
        out_shape=(
            jax.ShapeDtypeStruct(weights.shape, jnp.float32),
            jax.ShapeDtypeStruct((8, 128), jnp.float32),
        ),
        in_specs=[smem, smem, smem, vmem, vmem, item, item],
        out_specs=(item, pl.BlockSpec((8, 128), lambda i: (0, 0))),
        scratch_shapes=[plane, plane, plane, plane, pltpu.SMEM((1,), jnp.int32)],
        compiler_params=pltpu.CompilerParams(vmem_limit_bytes=48 << 20),
    )(counts, ridge, stats, high, low, weights, mask)


def misfit_kernel(experts, tokens, slots, payload_ref, out_ref, held, send_sem, recv_sem):
    devices = experts * tokens
    expert, token = lax.axis_index("expert"), lax.axis_index("token")
    me = expert * tokens + token
    barrier = pltpu.get_barrier_semaphore()

    def peer_of(offset):
        peer = lax.rem(me + offset, devices)
        return (lax.div(peer, tokens), lax.rem(peer, tokens))

    @pl.loop(1, devices)
    def _(offset):
        pl.semaphore_signal(barrier, inc=1, device_id=peer_of(offset), device_id_type=MESH)

    pl.semaphore_wait(barrier, devices - 1)

    def copy(offset):
        return pltpu.make_async_remote_copy(
            src_ref=payload_ref,
            dst_ref=held.at[me],
            send_sem=send_sem.at[offset],
            recv_sem=recv_sem.at[offset],
            device_id=peer_of(offset),
            device_id_type=MESH,
        )

    @pl.loop(1, devices)
    def _(offset):
        copy(offset).start()

    held[me] = payload_ref[...]

    @pl.loop(1, devices)
    def _(offset):
        copy(offset).wait_recv()

    energy = jnp.sum(held[...], axis=0)[0:1, :]
    numerator = jnp.sum(held[pl.ds(expert * tokens, tokens)], axis=0)[1:2, :]
    out_ref[...] = numerator / (energy / (slots * experts) + 1e-06)

    @pl.loop(1, devices)
    def _(offset):
        copy(offset).wait_send()


def misfit_call(experts, tokens, slots, payload):
    devices = experts * tokens
    vmem = pl.BlockSpec(memory_space=pltpu.VMEM)
    return pl.pallas_call(
        functools.partial(misfit_kernel, experts, tokens, slots),
        out_shape=jax.ShapeDtypeStruct((1, 128), jnp.float32),
        in_specs=[vmem],
        out_specs=vmem,
        scratch_shapes=[
            pltpu.VMEM((devices, 8, 128), jnp.float32),
            pltpu.SemaphoreType.DMA((devices,)),
            pltpu.SemaphoreType.DMA((devices,)),
        ],
        compiler_params=pltpu.CompilerParams(collective_id=1, has_side_effects=True),
    )(payload)


def on_device(experts, tokens, activations, routed, weights, kept_mask, step_counts, ridge_scale):
    slots = activations.shape[0]
    group = (D // COLS) // weights.shape[0]
    masked = activations * routed[:, :, None].astype(jnp.bfloat16)
    high, low, stats = gram_call(tokens, group, masked, weights)
    rebuilt, payload = solve_call(
        group, step_counts, ridge_scale, stats, high, low, weights, kept_mask
    )
    misfit = misfit_call(experts, tokens, slots, payload)[0, :slots]
    return (rebuilt, misfit)


def solution(mesh):
    placed = (
        P("expert", "token", None),
        P("expert", "token"),
        P(("expert", "token"), None, None),
        P(("expert", "token"), None, None),
        P(("expert", "token")),
        P(("expert", "token")),
    )
    return jax.shard_map(
        functools.partial(on_device, mesh.shape["expert"], mesh.shape["token"]),
        mesh=mesh,
        in_specs=placed,
        out_specs=(P(("expert", "token"), None, None), P("expert")),
        check_vma=False,
    )
```

```python
import functools

import jax
import jax.numpy as jnp
from jax import lax
from jax.experimental import pallas as pl
from jax.experimental.pallas import tpu as pltpu
from jax.sharding import PartitionSpec as P

D = 2048
COLS = 256
MESH = pl.DeviceIdType.MESH
PASSES = 3
MOST_STEPS = 7


def dot(a, b):
    return jnp.dot(a, b, preferred_element_type=jnp.float32)


def split(value):
    high = value.astype(jnp.bfloat16)
    return high, (value - high.astype(jnp.float32)).astype(jnp.bfloat16)


def solve_kernel(
    experts, tokens, group, x_ref, routed_ref, counts_ref, ridge_ref, w_hbm, mask_hbm,
    rebuilt_hbm, misfit_ref,
    recv, routes, total, outer, high_ref, low_ref, w_buf, mask_buf, out_buf, energies, numerators,
    payload, planes, load_sem, out_sem, send_sem, recv_sem, route_send, route_recv,
    energy_send, energy_recv, numer_send, numer_recv,
):
    slots, rows, features = x_ref.shape
    tasks, _, columns = w_buf.shape
    block = features // 3 if features % 384 == 0 else features
    devices = experts * tokens
    expert, me = lax.axis_index("expert"), lax.axis_index("token")
    place_of_me = expert * tokens + me
    own = me // group
    loads = [
        pltpu.make_async_copy(w_hbm, w_buf, load_sem.at[0]),
        pltpu.make_async_copy(mask_hbm, mask_buf, load_sem.at[1]),
    ]
    for load in loads:
        load.start()

    has_left = me > 0
    has_right = me < tokens - 1
    barrier = pltpu.get_barrier_semaphore()

    def peer_of(offset):
        peer = lax.rem(place_of_me + offset, devices)
        return (lax.div(peer, tokens), lax.rem(peer, tokens))

    @pl.loop(1, devices)
    def _(offset):
        pl.semaphore_signal(barrier, inc=1, device_id=peer_of(offset), device_id_type=MESH)

    pl.semaphore_wait(barrier, devices - 1)

    def line_copy(offset, source, target, send, receive):
        return pltpu.make_async_remote_copy(
            src_ref=source,
            dst_ref=target,
            send_sem=send.at[offset],
            recv_sem=receive.at[offset],
            device_id={"token": lax.rem(me + offset, tokens)},
            device_id_type=MESH,
        )

    def sends(way, k, slot):
        if way == 0:
            return has_right & (me - k >= 0) & ((slot + 1) * group - 1 >= me + 1)
        return has_left & (me + k < tokens) & (slot * group <= me - 1)

    def receives(way, k, slot):
        if way == 0:
            return (me - 1 - k >= 0) & ((slot + 1) * group - 1 >= me)
        return (me + 1 + k < tokens) & (slot * group <= me)

    def copy(way, k, slot, source, origin):
        return pltpu.make_async_remote_copy(
            src_ref=source,
            dst_ref=recv.at[slot, origin],
            send_sem=send_sem.at[way, k, slot],
            recv_sem=recv_sem.at[way, k, slot],
            device_id={"token": me + 1 if way == 0 else me - 1},
            device_id_type=MESH,
        )

    def slot_order(way):
        return range(slots - 1, -1, -1) if way == 0 else range(slots)

    def add_gram(rows_ref, route):
        value = rows_ref[...]
        left = value.T * route.astype(jnp.float32).astype(jnp.bfloat16)
        for start in range(0, features, block):
            total[start : start + block, :] += dot(left[start : start + block, :], value)

    for place in range(slots):
        for way in range(2):
            slot = list(slot_order(way))[place]

            @pl.when(sends(way, 0, slot))
            def _(way=way, slot=slot):
                copy(way, 0, slot, x_ref.at[slot], me).start()

        if place == 0:

            @pl.loop(1, tokens)
            def _(offset):
                line_copy(offset, routed_ref, routes.at[me], route_send, route_recv).start()

    total[...] = jnp.zeros_like(total)
    add_gram(x_ref.at[own], routed_ref[pl.ds(own, 1), :])
    outer[...] = jnp.zeros_like(outer)
    for load in loads:
        load.wait()

    @pl.loop(0, tasks)
    def _(task):
        value = w_buf[task]
        for start in range(0, features, block):
            outer[start : start + block, :] += lax.dot_general(
                value[start : start + block, :], value, (((1,), (1,)), ((), ())),
                preferred_element_type=jnp.float32,
            )

    @pl.loop(1, tokens)
    def _(offset):
        line_copy(offset, routed_ref, routes.at[me], route_send, route_recv).wait_recv()

    def origin_of(way, k):
        return me - 1 - k if way == 0 else me + 1 + k

    @pl.loop(0, tokens - 1)
    def _(k):
        for place in range(slots):
            for way in range(2):
                slot = list(slot_order(way))[place]
                origin = origin_of(way, k)

                @pl.when(sends(way, k + 1, slot))
                def _(way=way, slot=slot, origin=origin):
                    copy(way, k, slot, x_ref.at[slot], origin).wait_recv()
                    copy(way, k + 1, slot, recv.at[slot, origin], origin).start()

        for way in range(2):

            @pl.when(sends(way, k + 1, own))
            def _(way=way):
                origin = origin_of(way, k)
                add_gram(recv.at[own, origin], routes[origin, pl.ds(own, 1), :])

    @pl.loop(0, tokens - 1)
    def _(k):
        for way in range(2):

            @pl.when(receives(way, k, own) & jnp.logical_not(sends(way, k + 1, own)))
            def _(way=way):
                origin = origin_of(way, k)
                copy(way, k, own, x_ref.at[own], origin).wait_recv()
                add_gram(recv.at[own, origin], routes[origin, pl.ds(own, 1), :])

    scale = 1.0 / (rows * tokens)
    square = jnp.zeros((1, features), jnp.float32)
    energy = jnp.zeros((1, features), jnp.float32)
    piece = block // 4
    for start in range(0, features, piece):
        part = total[start : start + piece, :] * scale
        high, low = split(part)
        high_ref[start : start + piece, :] = high
        low_ref[start : start + piece, :] = low
        square = square + jnp.sum(part * part, axis=0, keepdims=True)
        energy = energy + jnp.sum(part * outer[start : start + piece, :], axis=0, keepdims=True)
    payload[0] = jnp.full(payload.shape[1:], jnp.sum(energy), jnp.float32)
    row = (1, columns)
    frobenius = jnp.sqrt(jnp.full(row, jnp.sum(square), jnp.float32))

    def rates(task):
        damping = ridge_ref[task] * frobenius
        step = 1.0 / (frobenius + damping)
        return step, step * damping

    def times_gram(value):
        if PASSES == 1:
            return dot(high_ref[...], value.astype(jnp.bfloat16))
        right_high, right_low = split(value)
        result = dot(high_ref[...], right_high) + dot(low_ref[...], right_high)
        if PASSES >= 3:
            result += dot(high_ref[...], right_low)
        return result

    width = planes.shape[0]
    delta, first, cross, scaled = (
        [planes.at[j, part] for j in range(width)] for part in range(4)
    )

    def begin(task, j):
        step, shrink = rates(task)
        kept = mask_buf[task] != 0
        weight = w_buf[task]
        pruned = jnp.where(kept, jnp.zeros_like(weight), weight)
        product = dot(high_ref[...], pruned) + dot(low_ref[...], pruned)
        cross[j][...] = product
        start = jnp.where(kept, step * product - shrink * weight.astype(jnp.float32), 0.0)
        first[j][...] = start
        delta[j][...] = start
        scaled[j][...] = jnp.where(kept, step, 0.0)

    def energy_copy(offset):
        return pltpu.make_async_remote_copy(
            src_ref=payload.at[0],
            dst_ref=energies.at[place_of_me],
            send_sem=energy_send.at[offset],
            recv_sem=energy_recv.at[offset],
            device_id=peer_of(offset),
            device_id_type=MESH,
        )

    def out_copy(task):
        return pltpu.make_async_copy(out_buf.at[task], rebuilt_hbm.at[task], out_sem.at[task])

    def advance(tasks_now):
        def turn_of(turn):
            products = [times_gram(delta[j][...]) for j in range(width)]
            for j in range(width):
                step, shrink = rates(tasks_now[j])
                active = jnp.full(row, turn, jnp.int32) < counts_ref[tasks_now[j]]
                keep = jnp.where(active, 1.0 - shrink, 1.0)
                push = jnp.where(active, 1.0, 0.0)
                delta[j][...] = (
                    keep * delta[j][...]
                    + push * (first[j][...] - scaled[j][...] * products[j])
                )

        pl.loop(1, MOST_STEPS)(turn_of)

    def finish(tasks_now, lines):
        amount = jnp.zeros(row, jnp.float32)
        for j in range(width):
            product = times_gram(delta[j][...])
            kept = mask_buf[tasks_now[j]] != 0
            weight = w_buf[tasks_now[j]].astype(jnp.float32)
            change = delta[j][...] - jnp.where(kept, 0.0, weight)
            amount = amount + jnp.sum(change * (product - cross[j][...]), axis=0, keepdims=True)
        lanes = lax.broadcasted_iota(jnp.int32, payload.shape[1:], 1)
        amount = jnp.where(lanes == own, jnp.sum(amount), 0.0)
        payload[1] = jnp.where(lines == 0, amount, payload[1] + amount)
        for j in range(width):
            kept = mask_buf[tasks_now[j]] != 0
            weight = w_buf[tasks_now[j]].astype(jnp.float32)
            out_buf[tasks_now[j]] = delta[j][...] + jnp.where(kept, weight, 0.0)
            out_copy(tasks_now[j]).start()

    payload[1] = jnp.zeros(payload.shape[1:], jnp.float32)

    @pl.loop(0, tasks // width)
    def _(round_index):
        now = [round_index * width + j for j in range(width)]
        for j in range(width):
            begin(now[j], j)

        @pl.when(round_index == 0)
        def _():
            @pl.loop(1, devices)
            def _(offset):
                energy_copy(offset).start()

        advance(now)
        finish(now, jnp.full(payload.shape[1:], round_index, jnp.int32))

    @pl.loop(1, tokens)
    def _(offset):
        line_copy(offset, payload.at[1], numerators.at[me], numer_send, numer_recv).start()

    energies[place_of_me] = payload[0]
    numerators[me] = payload[1]

    @pl.loop(1, devices)
    def _(offset):
        energy_copy(offset).wait()

    layer = jnp.sum(energies[...], axis=0) / (slots * experts) + 1e-06

    @pl.loop(0, tokens - 1)
    def _(k):
        for way in range(2):
            for slot in range(slots):

                @pl.when(sends(way, k, slot))
                def _(way=way, slot=slot):
                    copy(way, k, slot, x_ref.at[slot], me).wait_send()

    @pl.loop(0, tasks)
    def _(task):
        out_copy(task).wait()

    @pl.loop(1, tokens)
    def _(offset):
        line_copy(offset, routed_ref, routes.at[me], route_send, route_recv).wait_send()
        line_copy(offset, payload.at[1], numerators.at[me], numer_send, numer_recv).wait()

    misfit_ref[...] = (jnp.sum(numerators[...], axis=0) / layer)[0:1, :]


def solve_call(experts, tokens, group, activations, routed, counts, ridge, weights, mask):
    slots, rows, features = activations.shape
    tasks, _, columns = weights.shape
    vmem = pl.BlockSpec(memory_space=pltpu.VMEM)
    smem = pl.BlockSpec(memory_space=pltpu.SMEM)
    left = pl.BlockSpec(memory_space=pl.ANY)
    devices = experts * tokens
    hops = max(tokens, 2)
    width = 2 if tasks % 2 == 0 else 1
    dma = pltpu.SemaphoreType.DMA
    square = (features, features)
    return pl.pallas_call(
        functools.partial(solve_kernel, experts, tokens, group),
        out_shape=(
            jax.ShapeDtypeStruct(weights.shape, jnp.float32),
            jax.ShapeDtypeStruct((1, 128), jnp.float32),
        ),
        in_specs=[vmem, vmem, smem, smem, left, left],
        out_specs=(left, vmem),
        scratch_shapes=[
            pltpu.VMEM((slots, tokens, rows, features), jnp.bfloat16),
            pltpu.VMEM((tokens, slots, rows), jnp.int32),
            pltpu.VMEM(square, jnp.float32),
            pltpu.VMEM(square, jnp.float32),
            pltpu.VMEM(square, jnp.bfloat16),
            pltpu.VMEM(square, jnp.bfloat16),
            pltpu.VMEM(weights.shape, weights.dtype),
            pltpu.VMEM(mask.shape, mask.dtype),
            pltpu.VMEM(weights.shape, jnp.float32),
            pltpu.VMEM((devices, 8, 128), jnp.float32),
            pltpu.VMEM((tokens, 8, 128), jnp.float32),
            pltpu.VMEM((2, 8, 128), jnp.float32),
            pltpu.VMEM((width, 4, features, columns), jnp.float32),
            dma((2,)),
            dma((tasks,)),
            dma((2, hops, slots)),
            dma((2, hops, slots)),
            dma((hops,)),
            dma((hops,)),
            dma((devices,)),
            dma((devices,)),
            dma((hops,)),
            dma((hops,)),
        ],
        compiler_params=pltpu.CompilerParams(
            collective_id=0, has_side_effects=True, vmem_limit_bytes=60 << 20
        ),
    )(activations, routed, counts, ridge, weights, mask)


def on_device(experts, tokens, activations, routed, weights, kept_mask, step_counts, ridge_scale):
    slots = activations.shape[0]
    group = (D // COLS) // weights.shape[0]
    rebuilt, misfit = solve_call(
        experts, tokens, group, activations, routed, step_counts, ridge_scale, weights, kept_mask
    )
    return (rebuilt, misfit[0, :slots])


def solution(mesh):
    placed = (
        P("expert", "token", None),
        P("expert", "token"),
        P(("expert", "token"), None, None),
        P(("expert", "token"), None, None),
        P(("expert", "token")),
        P(("expert", "token")),
    )
    return jax.shard_map(
        functools.partial(on_device, mesh.shape["expert"], mesh.shape["token"]),
        mesh=mesh,
        in_specs=placed,
        out_specs=(P(("expert", "token"), None, None), P("expert")),
        check_vma=False,
    )
```

```python
import functools

import jax
import jax.numpy as jnp
from jax import lax
from jax.experimental import pallas as pl
from jax.experimental.pallas import tpu as pltpu
from jax.sharding import PartitionSpec as P

D = 2048
COLS = 256
MESH = pl.DeviceIdType.MESH


def dot(a, b):
    return jnp.dot(a, b, preferred_element_type=jnp.float32)


def split(value):
    high = value.astype(jnp.bfloat16)
    return high, (value - high.astype(jnp.float32)).astype(jnp.bfloat16)


def gram_kernel(
    tokens, group, x_ref, routed_ref, w_hbm, high_ref, low_ref, stats_ref,
    recv, routes, total, outer, w_buf, w_sem, send_sem, recv_sem, route_send, route_recv,
):
    slots, rows, features = x_ref.shape
    block = features // 3 if features % 384 == 0 else features
    me = lax.axis_index("token")
    own = me // group
    load = pltpu.make_async_copy(w_hbm, w_buf, w_sem)
    load.start()

    has_left = me > 0
    has_right = me < tokens - 1
    barrier = pltpu.get_barrier_semaphore()

    @pl.loop(1, tokens)
    def _(offset):
        pl.semaphore_signal(
            barrier, inc=1, device_id={"token": lax.rem(me + offset, tokens)}, device_id_type=MESH
        )

    pl.semaphore_wait(barrier, tokens - 1)

    def route_copy(offset):
        return pltpu.make_async_remote_copy(
            src_ref=routed_ref,
            dst_ref=routes.at[me],
            send_sem=route_send.at[offset],
            recv_sem=route_recv.at[offset],
            device_id={"token": lax.rem(me + offset, tokens)},
            device_id_type=MESH,
        )

    def sends(way, k, slot):
        if way == 0:
            return has_right & (me - k >= 0) & ((slot + 1) * group - 1 >= me + 1)
        return has_left & (me + k < tokens) & (slot * group <= me - 1)

    def receives(way, k, slot):
        if way == 0:
            return (me - 1 - k >= 0) & ((slot + 1) * group - 1 >= me)
        return (me + 1 + k < tokens) & (slot * group <= me)

    def copy(way, k, slot, source, origin):
        return pltpu.make_async_remote_copy(
            src_ref=source,
            dst_ref=recv.at[slot, origin],
            send_sem=send_sem.at[way, k, slot],
            recv_sem=recv_sem.at[way, k, slot],
            device_id={"token": me + 1 if way == 0 else me - 1},
            device_id_type=MESH,
        )

    def slot_order(way):
        return range(slots - 1, -1, -1) if way == 0 else range(slots)

    def add_gram(rows_ref, route):
        value = rows_ref[...]
        left = value.T * route.astype(jnp.float32).astype(jnp.bfloat16)
        for start in range(0, features, block):
            total[start : start + block, :] += dot(left[start : start + block, :], value)

    for place in range(slots):
        for way in range(2):
            slot = list(slot_order(way))[place]

            @pl.when(sends(way, 0, slot))
            def _(way=way, slot=slot):
                copy(way, 0, slot, x_ref.at[slot], me).start()

        if place == 0:

            @pl.loop(1, tokens)
            def _(offset):
                route_copy(offset).start()

    total[...] = jnp.zeros_like(total)
    add_gram(x_ref.at[own], routed_ref[pl.ds(own, 1), :])
    outer[...] = jnp.zeros_like(outer)
    load.wait()

    @pl.loop(0, w_buf.shape[0])
    def _(task):
        value = w_buf[task]
        for start in range(0, features, block):
            outer[start : start + block, :] += lax.dot_general(
                value[start : start + block, :], value, (((1,), (1,)), ((), ())),
                preferred_element_type=jnp.float32,
            )

    @pl.loop(1, tokens)
    def _(offset):
        route_copy(offset).wait_recv()

    def origin_of(way, k):
        return me - 1 - k if way == 0 else me + 1 + k

    @pl.loop(0, tokens - 1)
    def _(k):
        for place in range(slots):
            for way in range(2):
                slot = list(slot_order(way))[place]
                origin = origin_of(way, k)

                @pl.when(sends(way, k + 1, slot))
                def _(way=way, slot=slot, origin=origin):
                    copy(way, k, slot, x_ref.at[slot], origin).wait_recv()
                    copy(way, k + 1, slot, recv.at[slot, origin], origin).start()

        for way in range(2):

            @pl.when(sends(way, k + 1, own))
            def _(way=way):
                origin = origin_of(way, k)
                add_gram(recv.at[own, origin], routes[origin, pl.ds(own, 1), :])

    @pl.loop(0, tokens - 1)
    def _(k):
        for way in range(2):

            @pl.when(receives(way, k, own) & jnp.logical_not(sends(way, k + 1, own)))
            def _(way=way):
                origin = origin_of(way, k)
                copy(way, k, own, x_ref.at[own], origin).wait_recv()
                add_gram(recv.at[own, origin], routes[origin, pl.ds(own, 1), :])

    scale = 1.0 / (rows * tokens)
    square = jnp.zeros((1, features), jnp.float32)
    energy = jnp.zeros((1, features), jnp.float32)
    piece = block // 4
    for start in range(0, features, piece):
        part = total[start : start + piece, :] * scale
        high, low = split(part)
        high_ref[start : start + piece, :] = high
        low_ref[start : start + piece, :] = low
        square = square + jnp.sum(part * part, axis=0, keepdims=True)
        energy = energy + jnp.sum(part * outer[start : start + piece, :], axis=0, keepdims=True)
    stats_ref[0] = jnp.sum(square)
    stats_ref[1] = jnp.sum(energy)

    @pl.loop(0, tokens - 1)
    def _(k):
        for way in range(2):
            for slot in range(slots):

                @pl.when(sends(way, k, slot))
                def _(way=way, slot=slot):
                    copy(way, k, slot, x_ref.at[slot], me).wait_send()

    @pl.loop(1, tokens)
    def _(offset):
        route_copy(offset).wait_send()


def gram_call(tokens, group, activations, routed, weights):
    slots, rows, features = activations.shape
    vmem = pl.BlockSpec(memory_space=pltpu.VMEM)
    hops = max(tokens, 2)
    return pl.pallas_call(
        functools.partial(gram_kernel, tokens, group),
        out_shape=(
            jax.ShapeDtypeStruct((features, features), jnp.bfloat16),
            jax.ShapeDtypeStruct((features, features), jnp.bfloat16),
            jax.ShapeDtypeStruct((2,), jnp.float32),
        ),
        in_specs=[vmem, vmem, pl.BlockSpec(memory_space=pl.ANY)],
        out_specs=(vmem, vmem, pl.BlockSpec(memory_space=pltpu.SMEM)),
        scratch_shapes=[
            pltpu.VMEM((slots, tokens, rows, features), jnp.bfloat16),
            pltpu.VMEM((tokens, slots, rows), jnp.int32),
            pltpu.VMEM((features, features), jnp.float32),
            pltpu.VMEM((features, features), jnp.float32),
            pltpu.VMEM(weights.shape, weights.dtype),
            pltpu.SemaphoreType.DMA,
            pltpu.SemaphoreType.DMA((2, hops, slots)),
            pltpu.SemaphoreType.DMA((2, hops, slots)),
            pltpu.SemaphoreType.DMA((hops,)),
            pltpu.SemaphoreType.DMA((hops,)),
        ],
        compiler_params=pltpu.CompilerParams(
            collective_id=0, has_side_effects=True, vmem_limit_bytes=48 << 20
        ),
    )(activations, routed, weights)


def solve_kernel(
    group, counts_ref, ridge_ref, stats_ref, high_ref, low_ref, w_ref, mask_ref,
    out_ref, payload_ref, delta, change, pending, cross,
):
    task = pl.program_id(0)
    features, columns = delta.shape
    block = features // 3 if features % 384 == 0 else features
    starts = range(0, features, block)
    row = (1, columns)
    frobenius = jnp.sqrt(jnp.full(row, stats_ref[0], jnp.float32))
    damping = ridge_ref[task] * frobenius
    step = 1.0 / (frobenius + damping)
    shrink = step * damping

    def times_gram(at, right):
        return dot(high_ref[at, :], right) + dot(low_ref[at, :], right)

    pruned = jnp.where(mask_ref[0] == 0, w_ref[0], jnp.zeros_like(w_ref[0]))
    for start in starts:
        at = slice(start, start + block)
        product = times_gram(at, pruned)
        cross[at, :] = product
        begin = jnp.where(
            mask_ref[0, at, :] != 0,
            step * product - shrink * w_ref[0, at, :].astype(jnp.float32),
            0.0,
        )
        delta[at, :] = begin
        change[at, :] = begin
        pending[at, :] = begin

    @pl.loop(1, counts_ref[task])
    def _(turn):
        right = pending[...].astype(jnp.bfloat16)
        for start in starts:
            at = slice(start, start + block)
            product = times_gram(at, right)
            left_out = pending[at, :] - right[at, :].astype(jnp.float32)
            fresh = (1.0 - shrink) * delta[at, :] - jnp.where(
                mask_ref[0, at, :] != 0, step * product, 0.0
            )
            delta[at, :] = fresh
            change[at, :] += fresh
            pending[at, :] = fresh + left_out

    right_high, right_low = split(change[...])
    numerator = jnp.zeros(row, jnp.float32)
    for start in starts:
        at = slice(start, start + block)
        product = times_gram(at, right_high) + dot(high_ref[at, :], right_low)
        weight = w_ref[0, at, :].astype(jnp.float32)
        kept = mask_ref[0, at, :] != 0
        out_ref[0, at, :] = change[at, :] + jnp.where(kept, weight, 0.0)
        numerator = numerator + jnp.sum(
            (change[at, :] - jnp.where(kept, 0.0, weight)) * (product - cross[at, :]),
            axis=0, keepdims=True,
        )

    own = lax.axis_index("token") // group
    lanes = lax.broadcasted_iota(jnp.int32, payload_ref.shape, 1)
    lines = lax.broadcasted_iota(jnp.int32, payload_ref.shape, 0)

    @pl.when(task == 0)
    def _():
        payload_ref[...] = jnp.where(lines == 0, stats_ref[1], 0.0)

    payload_ref[...] += jnp.where((lines == 1) & (lanes == own), jnp.sum(numerator), 0.0)


def solve_call(group, counts, ridge, stats, high, low, weights, mask):
    tasks, features, columns = weights.shape
    smem = pl.BlockSpec(memory_space=pltpu.SMEM)
    vmem = pl.BlockSpec(memory_space=pltpu.VMEM)
    item = pl.BlockSpec((1, features, columns), lambda i: (i, 0, 0))
    plane = pltpu.VMEM((features, columns), jnp.float32)
    return pl.pallas_call(
        functools.partial(solve_kernel, group),
        grid=(tasks,),
        out_shape=(
            jax.ShapeDtypeStruct(weights.shape, jnp.float32),
            jax.ShapeDtypeStruct((8, 128), jnp.float32),
        ),
        in_specs=[smem, smem, smem, vmem, vmem, item, item],
        out_specs=(item, pl.BlockSpec((8, 128), lambda i: (0, 0))),
        scratch_shapes=[plane, plane, plane, plane],
        compiler_params=pltpu.CompilerParams(vmem_limit_bytes=48 << 20),
    )(counts, ridge, stats, high, low, weights, mask)


def misfit_kernel(experts, tokens, slots, payload_ref, out_ref, held, send_sem, recv_sem):
    devices = experts * tokens
    expert, token = lax.axis_index("expert"), lax.axis_index("token")
    me = expert * tokens + token
    barrier = pltpu.get_barrier_semaphore()

    def peer_of(offset):
        peer = lax.rem(me + offset, devices)
        return (lax.div(peer, tokens), lax.rem(peer, tokens))

    @pl.loop(1, devices)
    def _(offset):
        pl.semaphore_signal(barrier, inc=1, device_id=peer_of(offset), device_id_type=MESH)

    pl.semaphore_wait(barrier, devices - 1)

    def copy(offset):
        return pltpu.make_async_remote_copy(
            src_ref=payload_ref,
            dst_ref=held.at[me],
            send_sem=send_sem.at[offset],
            recv_sem=recv_sem.at[offset],
            device_id=peer_of(offset),
            device_id_type=MESH,
        )

    @pl.loop(1, devices)
    def _(offset):
        copy(offset).start()

    held[me] = payload_ref[...]

    @pl.loop(1, devices)
    def _(offset):
        copy(offset).wait_recv()

    energy = jnp.sum(held[...], axis=0)[0:1, :]
    numerator = jnp.sum(held[pl.ds(expert * tokens, tokens)], axis=0)[1:2, :]
    out_ref[...] = numerator / (energy / (slots * experts) + 1e-06)

    @pl.loop(1, devices)
    def _(offset):
        copy(offset).wait_send()


def misfit_call(experts, tokens, slots, payload):
    devices = experts * tokens
    vmem = pl.BlockSpec(memory_space=pltpu.VMEM)
    return pl.pallas_call(
        functools.partial(misfit_kernel, experts, tokens, slots),
        out_shape=jax.ShapeDtypeStruct((1, 128), jnp.float32),
        in_specs=[vmem],
        out_specs=vmem,
        scratch_shapes=[
            pltpu.VMEM((devices, 8, 128), jnp.float32),
            pltpu.SemaphoreType.DMA((devices,)),
            pltpu.SemaphoreType.DMA((devices,)),
        ],
        compiler_params=pltpu.CompilerParams(collective_id=1, has_side_effects=True),
    )(payload)


def on_device(experts, tokens, activations, routed, weights, kept_mask, step_counts, ridge_scale):
    slots = activations.shape[0]
    group = (D // COLS) // weights.shape[0]
    high, low, stats = gram_call(tokens, group, activations, routed, weights)
    rebuilt, payload = solve_call(
        group, step_counts, ridge_scale, stats, high, low, weights, kept_mask
    )
    misfit = misfit_call(experts, tokens, slots, payload)[0, :slots]
    return (rebuilt, misfit)


def solution(mesh):
    placed = (
        P("expert", "token", None),
        P("expert", "token"),
        P(("expert", "token"), None, None),
        P(("expert", "token"), None, None),
        P(("expert", "token")),
        P(("expert", "token")),
    )
    return jax.shard_map(
        functools.partial(on_device, mesh.shape["expert"], mesh.shape["token"]),
        mesh=mesh,
        in_specs=placed,
        out_specs=(P(("expert", "token"), None, None), P("expert")),
        check_vma=False,
    )
```

```python
import functools

import jax
import jax.numpy as jnp
from jax import lax
from jax.experimental import pallas as pl
from jax.experimental.pallas import tpu as pltpu
from jax.sharding import PartitionSpec as P

D = 2048
COLS = 256
MESH = pl.DeviceIdType.MESH


def dot(a, b):
    return jnp.dot(a, b, preferred_element_type=jnp.float32)


def split(value):
    high = value.astype(jnp.bfloat16)
    return high, (value - high.astype(jnp.float32)).astype(jnp.bfloat16)


def gram_kernel(
    tokens, group, x_ref, routed_ref, w_hbm, high_ref, low_ref, stats_ref,
    recv, own_rows, routes, total, outer, w_buf, own_sem, w_sem, send_sem, recv_sem, route_send, route_recv,
):
    slots, rows, features = x_ref.shape
    block = features // 3 if features % 384 == 0 else features
    me = lax.axis_index("token")
    own = me // group
    load_rows = pltpu.make_async_copy(x_ref.at[own], own_rows, own_sem)
    load_rows.start()
    load = pltpu.make_async_copy(w_hbm, w_buf, w_sem)
    load.start()

    has_left = me > 0
    has_right = me < tokens - 1
    barrier = pltpu.get_barrier_semaphore()

    @pl.loop(1, tokens)
    def _(offset):
        pl.semaphore_signal(
            barrier, inc=1, device_id={"token": lax.rem(me + offset, tokens)}, device_id_type=MESH
        )

    pl.semaphore_wait(barrier, tokens - 1)

    def route_copy(offset):
        return pltpu.make_async_remote_copy(
            src_ref=routed_ref,
            dst_ref=routes.at[me],
            send_sem=route_send.at[offset],
            recv_sem=route_recv.at[offset],
            device_id={"token": lax.rem(me + offset, tokens)},
            device_id_type=MESH,
        )

    def sends(way, k, slot):
        if way == 0:
            return has_right & (me - k >= 0) & ((slot + 1) * group - 1 >= me + 1)
        return has_left & (me + k < tokens) & (slot * group <= me - 1)

    def receives(way, k, slot):
        if way == 0:
            return (me - 1 - k >= 0) & ((slot + 1) * group - 1 >= me)
        return (me + 1 + k < tokens) & (slot * group <= me)

    def copy(way, k, slot, source, origin):
        return pltpu.make_async_remote_copy(
            src_ref=source,
            dst_ref=recv.at[slot, origin],
            send_sem=send_sem.at[way, k, slot],
            recv_sem=recv_sem.at[way, k, slot],
            device_id={"token": me + 1 if way == 0 else me - 1},
            device_id_type=MESH,
        )

    def slot_order(way):
        return range(slots - 1, -1, -1) if way == 0 else range(slots)

    def add_gram(rows_ref, route):
        value = rows_ref[...]
        left = value.T * route.astype(jnp.float32).astype(jnp.bfloat16)
        for start in range(0, features, block):
            total[start : start + block, :] += dot(left[start : start + block, :], value)

    for place in range(slots):
        for way in range(2):
            slot = list(slot_order(way))[place]

            @pl.when(sends(way, 0, slot))
            def _(way=way, slot=slot):
                copy(way, 0, slot, x_ref.at[slot], me).start()

        if place == 0:

            @pl.loop(1, tokens)
            def _(offset):
                route_copy(offset).start()

    total[...] = jnp.zeros_like(total)
    load_rows.wait()
    add_gram(own_rows, routed_ref[pl.ds(own, 1), :])
    outer[...] = jnp.zeros_like(outer)
    load.wait()

    @pl.loop(0, w_buf.shape[0])
    def _(task):
        value = w_buf[task]
        for start in range(0, features, block):
            outer[start : start + block, :] += lax.dot_general(
                value[start : start + block, :], value, (((1,), (1,)), ((), ())),
                preferred_element_type=jnp.float32,
            )

    @pl.loop(1, tokens)
    def _(offset):
        route_copy(offset).wait_recv()

    def origin_of(way, k):
        return me - 1 - k if way == 0 else me + 1 + k

    @pl.loop(0, tokens - 1)
    def _(k):
        for place in range(slots):
            for way in range(2):
                slot = list(slot_order(way))[place]
                origin = origin_of(way, k)

                @pl.when(sends(way, k + 1, slot))
                def _(way=way, slot=slot, origin=origin):
                    copy(way, k, slot, x_ref.at[slot], origin).wait_recv()
                    copy(way, k + 1, slot, recv.at[slot, origin], origin).start()

        for way in range(2):

            @pl.when(sends(way, k + 1, own))
            def _(way=way):
                origin = origin_of(way, k)
                add_gram(recv.at[own, origin], routes[origin, pl.ds(own, 1), :])

    @pl.loop(0, tokens - 1)
    def _(k):
        for way in range(2):

            @pl.when(receives(way, k, own) & jnp.logical_not(sends(way, k + 1, own)))
            def _(way=way):
                origin = origin_of(way, k)
                copy(way, k, own, x_ref.at[own], origin).wait_recv()
                add_gram(recv.at[own, origin], routes[origin, pl.ds(own, 1), :])

    scale = 1.0 / (rows * tokens)
    square = jnp.zeros((1, features), jnp.float32)
    energy = jnp.zeros((1, features), jnp.float32)
    piece = block // 4
    for start in range(0, features, piece):
        part = total[start : start + piece, :] * scale
        high, low = split(part)
        high_ref[start : start + piece, :] = high
        low_ref[start : start + piece, :] = low
        square = square + jnp.sum(part * part, axis=0, keepdims=True)
        energy = energy + jnp.sum(part * outer[start : start + piece, :], axis=0, keepdims=True)
    stats_ref[0] = jnp.sum(square)
    stats_ref[1] = jnp.sum(energy)

    @pl.loop(0, tokens - 1)
    def _(k):
        for way in range(2):
            for slot in range(slots):

                @pl.when(sends(way, k, slot))
                def _(way=way, slot=slot):
                    copy(way, k, slot, x_ref.at[slot], me).wait_send()

    @pl.loop(1, tokens)
    def _(offset):
        route_copy(offset).wait_send()


def gram_call(tokens, group, activations, routed, weights):
    slots, rows, features = activations.shape
    vmem = pl.BlockSpec(memory_space=pltpu.VMEM)
    hops = max(tokens, 2)
    hbm = pl.BlockSpec(memory_space=pltpu.HBM)
    return pl.pallas_call(
        functools.partial(gram_kernel, tokens, group),
        out_shape=(
            jax.ShapeDtypeStruct((features, features), jnp.bfloat16),
            jax.ShapeDtypeStruct((features, features), jnp.bfloat16),
            jax.ShapeDtypeStruct((2,), jnp.float32),
        ),
        in_specs=[hbm, vmem, hbm],
        out_specs=(vmem, vmem, pl.BlockSpec(memory_space=pltpu.SMEM)),
        scratch_shapes=[
            pltpu.VMEM((slots, tokens, rows, features), jnp.bfloat16),
            pltpu.VMEM((rows, features), jnp.bfloat16),
            pltpu.VMEM((tokens, slots, rows), jnp.int32),
            pltpu.VMEM((features, features), jnp.float32),
            pltpu.VMEM((features, features), jnp.float32),
            pltpu.VMEM(weights.shape, weights.dtype),
            pltpu.SemaphoreType.DMA,
            pltpu.SemaphoreType.DMA,
            pltpu.SemaphoreType.DMA((2, hops, slots)),
            pltpu.SemaphoreType.DMA((2, hops, slots)),
            pltpu.SemaphoreType.DMA((hops,)),
            pltpu.SemaphoreType.DMA((hops,)),
        ],
        compiler_params=pltpu.CompilerParams(
            collective_id=0, has_side_effects=True, vmem_limit_bytes=62 << 20
        ),
    )(activations, routed, weights)


def solve_kernel(
    group, counts_ref, ridge_ref, stats_ref, high_ref, low_ref, w_ref, mask_ref,
    out_ref, payload_ref, delta, change, pending, cross,
):
    task = pl.program_id(0)
    features, columns = delta.shape
    block = features // 3 if features % 384 == 0 else features
    starts = range(0, features, block)
    row = (1, columns)
    frobenius = jnp.sqrt(jnp.full(row, stats_ref[0], jnp.float32))
    damping = ridge_ref[task] * frobenius
    step = 1.0 / (frobenius + damping)
    shrink = step * damping

    def times_gram(at, right):
        return dot(high_ref[at, :], right) + dot(low_ref[at, :], right)

    pruned = jnp.where(mask_ref[0] == 0, w_ref[0], jnp.zeros_like(w_ref[0]))
    for start in starts:
        at = slice(start, start + block)
        product = times_gram(at, pruned)
        cross[at, :] = product
        begin = jnp.where(
            mask_ref[0, at, :] != 0,
            step * product - shrink * w_ref[0, at, :].astype(jnp.float32),
            0.0,
        )
        delta[at, :] = begin
        change[at, :] = begin
        pending[at, :] = begin

    @pl.loop(1, counts_ref[task])
    def _(turn):
        right = pending[...].astype(jnp.bfloat16)
        for start in starts:
            at = slice(start, start + block)
            product = times_gram(at, right)
            left_out = pending[at, :] - right[at, :].astype(jnp.float32)
            fresh = (1.0 - shrink) * delta[at, :] - jnp.where(
                mask_ref[0, at, :] != 0, step * product, 0.0
            )
            delta[at, :] = fresh
            change[at, :] += fresh
            pending[at, :] = fresh + left_out

    right_high, right_low = split(change[...])
    numerator = jnp.zeros(row, jnp.float32)
    for start in starts:
        at = slice(start, start + block)
        product = times_gram(at, right_high) + dot(high_ref[at, :], right_low)
        weight = w_ref[0, at, :].astype(jnp.float32)
        kept = mask_ref[0, at, :] != 0
        out_ref[0, at, :] = change[at, :] + jnp.where(kept, weight, 0.0)
        numerator = numerator + jnp.sum(
            (change[at, :] - jnp.where(kept, 0.0, weight)) * (product - cross[at, :]),
            axis=0, keepdims=True,
        )

    own = lax.axis_index("token") // group
    lanes = lax.broadcasted_iota(jnp.int32, payload_ref.shape, 1)
    lines = lax.broadcasted_iota(jnp.int32, payload_ref.shape, 0)

    @pl.when(task == 0)
    def _():
        payload_ref[...] = jnp.where(lines == 0, stats_ref[1], 0.0)

    payload_ref[...] += jnp.where((lines == 1) & (lanes == own), jnp.sum(numerator), 0.0)


def solve_call(group, counts, ridge, stats, high, low, weights, mask):
    tasks, features, columns = weights.shape
    smem = pl.BlockSpec(memory_space=pltpu.SMEM)
    vmem = pl.BlockSpec(memory_space=pltpu.VMEM)
    item = pl.BlockSpec((1, features, columns), lambda i: (i, 0, 0))
    plane = pltpu.VMEM((features, columns), jnp.float32)
    return pl.pallas_call(
        functools.partial(solve_kernel, group),
        grid=(tasks,),
        out_shape=(
            jax.ShapeDtypeStruct(weights.shape, jnp.float32),
            jax.ShapeDtypeStruct((8, 128), jnp.float32),
        ),
        in_specs=[smem, smem, smem, vmem, vmem, item, item],
        out_specs=(item, pl.BlockSpec((8, 128), lambda i: (0, 0))),
        scratch_shapes=[plane, plane, plane, plane],
        compiler_params=pltpu.CompilerParams(vmem_limit_bytes=62 << 20),
    )(counts, ridge, stats, high, low, weights, mask)


def misfit_kernel(experts, tokens, slots, payload_ref, out_ref, held, send_sem, recv_sem):
    devices = experts * tokens
    expert, token = lax.axis_index("expert"), lax.axis_index("token")
    me = expert * tokens + token
    barrier = pltpu.get_barrier_semaphore()

    def peer_of(offset):
        peer = lax.rem(me + offset, devices)
        return (lax.div(peer, tokens), lax.rem(peer, tokens))

    @pl.loop(1, devices)
    def _(offset):
        pl.semaphore_signal(barrier, inc=1, device_id=peer_of(offset), device_id_type=MESH)

    pl.semaphore_wait(barrier, devices - 1)

    def copy(offset):
        return pltpu.make_async_remote_copy(
            src_ref=payload_ref,
            dst_ref=held.at[me],
            send_sem=send_sem.at[offset],
            recv_sem=recv_sem.at[offset],
            device_id=peer_of(offset),
            device_id_type=MESH,
        )

    @pl.loop(1, devices)
    def _(offset):
        copy(offset).start()

    held[me] = payload_ref[...]

    @pl.loop(1, devices)
    def _(offset):
        copy(offset).wait_recv()

    energy = jnp.sum(held[...], axis=0)[0:1, :]
    numerator = jnp.sum(held[pl.ds(expert * tokens, tokens)], axis=0)[1:2, :]
    out_ref[...] = numerator / (energy / (slots * experts) + 1e-06)

    @pl.loop(1, devices)
    def _(offset):
        copy(offset).wait_send()


def misfit_call(experts, tokens, slots, payload):
    devices = experts * tokens
    vmem = pl.BlockSpec(memory_space=pltpu.VMEM)
    return pl.pallas_call(
        functools.partial(misfit_kernel, experts, tokens, slots),
        out_shape=jax.ShapeDtypeStruct((1, 128), jnp.float32),
        in_specs=[vmem],
        out_specs=vmem,
        scratch_shapes=[
            pltpu.VMEM((devices, 8, 128), jnp.float32),
            pltpu.SemaphoreType.DMA((devices,)),
            pltpu.SemaphoreType.DMA((devices,)),
        ],
        compiler_params=pltpu.CompilerParams(collective_id=1, has_side_effects=True),
    )(payload)


def on_device(experts, tokens, activations, routed, weights, kept_mask, step_counts, ridge_scale):
    slots = activations.shape[0]
    group = (D // COLS) // weights.shape[0]
    high, low, stats = gram_call(tokens, group, activations, routed, weights)
    rebuilt, payload = solve_call(
        group, step_counts, ridge_scale, stats, high, low, weights, kept_mask
    )
    misfit = misfit_call(experts, tokens, slots, payload)[0, :slots]
    return (rebuilt, misfit)


def solution(mesh):
    placed = (
        P("expert", "token", None),
        P("expert", "token"),
        P(("expert", "token"), None, None),
        P(("expert", "token"), None, None),
        P(("expert", "token")),
        P(("expert", "token")),
    )
    return jax.shard_map(
        functools.partial(on_device, mesh.shape["expert"], mesh.shape["token"]),
        mesh=mesh,
        in_specs=placed,
        out_specs=(P(("expert", "token"), None, None), P("expert")),
        check_vma=False,
    )
```

```python
import functools

import jax
import jax.numpy as jnp
from jax import lax
from jax.experimental import pallas as pl
from jax.experimental.pallas import tpu as pltpu
from jax.sharding import PartitionSpec as P

D = 2048
COLS = 256
MESH = pl.DeviceIdType.MESH


def dot(a, b):
    return jnp.dot(a, b, preferred_element_type=jnp.float32)


def split(value):
    high = value.astype(jnp.bfloat16)
    return high, (value - high.astype(jnp.float32)).astype(jnp.bfloat16)


def gram_kernel(
    tokens, group, x_ref, routed_ref, w_hbm, high_ref, low_ref, stats_ref,
    recv, own_rows, routes, total, outer, w_buf, own_sem, w_sem, send_sem, recv_sem, route_send, route_recv,
):
    slots, rows, features = x_ref.shape
    block = features // 3 if features % 384 == 0 else features
    me = lax.axis_index("token")
    own = me // group
    load_rows = pltpu.make_async_copy(x_ref.at[own], own_rows, own_sem)
    load_rows.start()
    load = pltpu.make_async_copy(w_hbm, w_buf, w_sem)
    load.start()

    has_left = me > 0
    has_right = me < tokens - 1
    barrier = pltpu.get_barrier_semaphore()

    @pl.loop(1, tokens)
    def _(offset):
        pl.semaphore_signal(
            barrier, inc=1, device_id={"token": lax.rem(me + offset, tokens)}, device_id_type=MESH
        )

    pl.semaphore_wait(barrier, tokens - 1)

    def route_copy(offset):
        return pltpu.make_async_remote_copy(
            src_ref=routed_ref,
            dst_ref=routes.at[me],
            send_sem=route_send.at[offset],
            recv_sem=route_recv.at[offset],
            device_id={"token": lax.rem(me + offset, tokens)},
            device_id_type=MESH,
        )

    def sends(way, k, slot):
        if way == 0:
            return has_right & (me - k >= 0) & ((slot + 1) * group - 1 >= me + 1)
        return has_left & (me + k < tokens) & (slot * group <= me - 1)

    def receives(way, k, slot):
        if way == 0:
            return (me - 1 - k >= 0) & ((slot + 1) * group - 1 >= me)
        return (me + 1 + k < tokens) & (slot * group <= me)

    def copy(way, k, slot, source, origin):
        return pltpu.make_async_remote_copy(
            src_ref=source,
            dst_ref=recv.at[slot, origin],
            send_sem=send_sem.at[way, k, slot],
            recv_sem=recv_sem.at[way, k, slot],
            device_id={"token": me + 1 if way == 0 else me - 1},
            device_id_type=MESH,
        )

    def slot_order(way):
        return range(slots - 1, -1, -1) if way == 0 else range(slots)

    def add_gram(rows_ref, route):
        value = rows_ref[...]
        left = value.T * route.astype(jnp.float32).astype(jnp.bfloat16)
        for start in range(0, features, block):
            total[start : start + block, :] += dot(left[start : start + block, :], value)

    for place in range(slots):
        for way in range(2):
            slot = list(slot_order(way))[place]

            @pl.when(sends(way, 0, slot))
            def _(way=way, slot=slot):
                copy(way, 0, slot, x_ref.at[slot], me).start()

        if place == 0:

            @pl.loop(1, tokens)
            def _(offset):
                route_copy(offset).start()

    total[...] = jnp.zeros_like(total)
    load_rows.wait()
    add_gram(own_rows, routed_ref[pl.ds(own, 1), :])
    outer[...] = jnp.zeros_like(outer)
    load.wait()

    @pl.loop(0, w_buf.shape[0])
    def _(task):
        value = w_buf[task]
        for start in range(0, features, block):
            outer[start : start + block, :] += lax.dot_general(
                value[start : start + block, :], value, (((1,), (1,)), ((), ())),
                preferred_element_type=jnp.float32,
            )

    @pl.loop(1, tokens)
    def _(offset):
        route_copy(offset).wait_recv()

    def origin_of(way, k):
        return me - 1 - k if way == 0 else me + 1 + k

    @pl.loop(0, tokens - 1)
    def _(k):
        for place in range(slots):
            for way in range(2):
                slot = list(slot_order(way))[place]
                origin = origin_of(way, k)

                @pl.when(sends(way, k + 1, slot))
                def _(way=way, slot=slot, origin=origin):
                    copy(way, k, slot, x_ref.at[slot], origin).wait_recv()
                    copy(way, k + 1, slot, recv.at[slot, origin], origin).start()

        for way in range(2):

            @pl.when(sends(way, k + 1, own))
            def _(way=way):
                origin = origin_of(way, k)
                add_gram(recv.at[own, origin], routes[origin, pl.ds(own, 1), :])

    @pl.loop(0, tokens - 1)
    def _(k):
        for way in range(2):

            @pl.when(receives(way, k, own) & jnp.logical_not(sends(way, k + 1, own)))
            def _(way=way):
                origin = origin_of(way, k)
                copy(way, k, own, x_ref.at[own], origin).wait_recv()
                add_gram(recv.at[own, origin], routes[origin, pl.ds(own, 1), :])

    scale = 1.0 / (rows * tokens)
    square = jnp.zeros((1, features), jnp.float32)
    energy = jnp.zeros((1, features), jnp.float32)
    piece = block // 4
    for start in range(0, features, piece):
        part = total[start : start + piece, :] * scale
        high, low = split(part)
        high_ref[start : start + piece, :] = high
        low_ref[start : start + piece, :] = low
        square = square + jnp.sum(part * part, axis=0, keepdims=True)
        energy = energy + jnp.sum(part * outer[start : start + piece, :], axis=0, keepdims=True)
    stats_ref[0] = jnp.sum(square)
    stats_ref[1] = jnp.sum(energy)

    @pl.loop(0, tokens - 1)
    def _(k):
        for way in range(2):
            for slot in range(slots):

                @pl.when(sends(way, k, slot))
                def _(way=way, slot=slot):
                    copy(way, k, slot, x_ref.at[slot], me).wait_send()

    @pl.loop(1, tokens)
    def _(offset):
        route_copy(offset).wait_send()


def gram_call(tokens, group, activations, routed, weights):
    slots, rows, features = activations.shape
    vmem = pl.BlockSpec(memory_space=pltpu.VMEM)
    hops = max(tokens, 2)
    hbm = pl.BlockSpec(memory_space=pltpu.HBM)
    return pl.pallas_call(
        functools.partial(gram_kernel, tokens, group),
        out_shape=(
            jax.ShapeDtypeStruct((features, features), jnp.bfloat16),
            jax.ShapeDtypeStruct((features, features), jnp.bfloat16),
            jax.ShapeDtypeStruct((2,), jnp.float32),
        ),
        in_specs=[hbm, vmem, hbm],
        out_specs=(vmem, vmem, pl.BlockSpec(memory_space=pltpu.SMEM)),
        scratch_shapes=[
            pltpu.VMEM((slots, tokens, rows, features), jnp.bfloat16),
            pltpu.VMEM((rows, features), jnp.bfloat16),
            pltpu.VMEM((tokens, slots, rows), jnp.int32),
            pltpu.VMEM((features, features), jnp.float32),
            pltpu.VMEM((features, features), jnp.float32),
            pltpu.VMEM(weights.shape, weights.dtype),
            pltpu.SemaphoreType.DMA,
            pltpu.SemaphoreType.DMA,
            pltpu.SemaphoreType.DMA((2, hops, slots)),
            pltpu.SemaphoreType.DMA((2, hops, slots)),
            pltpu.SemaphoreType.DMA((hops,)),
            pltpu.SemaphoreType.DMA((hops,)),
        ],
        compiler_params=pltpu.CompilerParams(
            collective_id=0, has_side_effects=True, vmem_limit_bytes=62 << 20
        ),
    )(activations, routed, weights)


def solve_kernel(
    group, counts_ref, ridge_ref, stats_ref, high_ref, low_ref, w_ref, mask_ref,
    out_ref, payload_ref, delta, change, pending, cross,
):
    task = pl.program_id(0)
    features, columns = delta.shape
    block = features // 3 if features % 384 == 0 else features
    starts = range(0, features, block)
    row = (1, columns)
    frobenius = jnp.sqrt(jnp.full(row, stats_ref[0], jnp.float32))
    damping = ridge_ref[task] * frobenius
    step = 1.0 / (frobenius + damping)
    shrink = step * damping

    def times_gram(at, right):
        return dot(high_ref[at, :], right) + dot(low_ref[at, :], right)

    pruned = jnp.where(mask_ref[0] == 0, w_ref[0], jnp.zeros_like(w_ref[0]))
    for start in starts:
        at = slice(start, start + block)
        product = times_gram(at, pruned)
        cross[at, :] = product
        begin = jnp.where(
            mask_ref[0, at, :] != 0,
            step * product - shrink * w_ref[0, at, :].astype(jnp.float32),
            0.0,
        )
        delta[at, :] = begin
        change[at, :] = begin
        pending[at, :] = begin

    @pl.loop(1, counts_ref[task])
    def _(turn):
        right = pending[...].astype(jnp.bfloat16)
        for start in starts:
            at = slice(start, start + block)
            product = times_gram(at, right)
            left_out = pending[at, :] - right[at, :].astype(jnp.float32)
            fresh = (1.0 - shrink) * delta[at, :] - jnp.where(
                mask_ref[0, at, :] != 0, step * product, 0.0
            )
            delta[at, :] = fresh
            change[at, :] += fresh
            pending[at, :] = fresh + left_out

    right_high, right_low = split(change[...])
    numerator = jnp.zeros(row, jnp.float32)
    for start in starts:
        at = slice(start, start + block)
        product = times_gram(at, right_high) + dot(high_ref[at, :], right_low)
        weight = w_ref[0, at, :].astype(jnp.float32)
        kept = mask_ref[0, at, :] != 0
        out_ref[0, at, :] = change[at, :] + jnp.where(kept, weight, 0.0)
        numerator = numerator + jnp.sum(
            (change[at, :] - jnp.where(kept, 0.0, weight)) * (product - cross[at, :]),
            axis=0, keepdims=True,
        )

    own = lax.axis_index("token") // group
    lanes = lax.broadcasted_iota(jnp.int32, payload_ref.shape, 1)
    lines = lax.broadcasted_iota(jnp.int32, payload_ref.shape, 0)

    @pl.when(task == 0)
    def _():
        payload_ref[...] = jnp.where(lines == 0, stats_ref[1], 0.0)

    payload_ref[...] += jnp.where((lines == 1) & (lanes == own), jnp.sum(numerator), 0.0)


def solve_call(group, counts, ridge, stats, high, low, weights, mask):
    tasks, features, columns = weights.shape
    smem = pl.BlockSpec(memory_space=pltpu.SMEM)
    vmem = pl.BlockSpec(memory_space=pltpu.VMEM)
    item = pl.BlockSpec((1, features, columns), lambda i: (i, 0, 0))
    plane = pltpu.VMEM((features, columns), jnp.float32)
    return pl.pallas_call(
        functools.partial(solve_kernel, group),
        grid=(tasks,),
        out_shape=(
            jax.ShapeDtypeStruct(weights.shape, jnp.float32),
            jax.ShapeDtypeStruct((8, 128), jnp.float32),
        ),
        in_specs=[smem, smem, smem, vmem, vmem, item, item],
        out_specs=(item, pl.BlockSpec((8, 128), lambda i: (0, 0))),
        scratch_shapes=[plane, plane, plane, plane],
        compiler_params=pltpu.CompilerParams(vmem_limit_bytes=48 << 20),
    )(counts, ridge, stats, high, low, weights, mask)


def misfit_kernel(experts, tokens, slots, payload_ref, out_ref, held, send_sem, recv_sem):
    devices = experts * tokens
    expert, token = lax.axis_index("expert"), lax.axis_index("token")
    me = expert * tokens + token
    barrier = pltpu.get_barrier_semaphore()

    def peer_of(offset):
        peer = lax.rem(me + offset, devices)
        return (lax.div(peer, tokens), lax.rem(peer, tokens))

    @pl.loop(1, devices)
    def _(offset):
        pl.semaphore_signal(barrier, inc=1, device_id=peer_of(offset), device_id_type=MESH)

    pl.semaphore_wait(barrier, devices - 1)

    def copy(offset):
        return pltpu.make_async_remote_copy(
            src_ref=payload_ref,
            dst_ref=held.at[me],
            send_sem=send_sem.at[offset],
            recv_sem=recv_sem.at[offset],
            device_id=peer_of(offset),
            device_id_type=MESH,
        )

    @pl.loop(1, devices)
    def _(offset):
        copy(offset).start()

    held[me] = payload_ref[...]

    @pl.loop(1, devices)
    def _(offset):
        copy(offset).wait_recv()

    energy = jnp.sum(held[...], axis=0)[0:1, :]
    numerator = jnp.sum(held[pl.ds(expert * tokens, tokens)], axis=0)[1:2, :]
    out_ref[...] = numerator / (energy / (slots * experts) + 1e-06)

    @pl.loop(1, devices)
    def _(offset):
        copy(offset).wait_send()


def misfit_call(experts, tokens, slots, payload):
    devices = experts * tokens
    vmem = pl.BlockSpec(memory_space=pltpu.VMEM)
    return pl.pallas_call(
        functools.partial(misfit_kernel, experts, tokens, slots),
        out_shape=jax.ShapeDtypeStruct((1, 128), jnp.float32),
        in_specs=[vmem],
        out_specs=vmem,
        scratch_shapes=[
            pltpu.VMEM((devices, 8, 128), jnp.float32),
            pltpu.SemaphoreType.DMA((devices,)),
            pltpu.SemaphoreType.DMA((devices,)),
        ],
        compiler_params=pltpu.CompilerParams(collective_id=1, has_side_effects=True),
    )(payload)


def on_device(experts, tokens, activations, routed, weights, kept_mask, step_counts, ridge_scale):
    slots = activations.shape[0]
    group = (D // COLS) // weights.shape[0]
    high, low, stats = gram_call(tokens, group, activations, routed, weights)
    rebuilt, payload = solve_call(
        group, step_counts, ridge_scale, stats, high, low, weights, kept_mask
    )
    misfit = misfit_call(experts, tokens, slots, payload)[0, :slots]
    return (rebuilt, misfit)


def solution(mesh):
    placed = (
        P("expert", "token", None),
        P("expert", "token"),
        P(("expert", "token"), None, None),
        P(("expert", "token"), None, None),
        P(("expert", "token")),
        P(("expert", "token")),
    )
    return jax.shard_map(
        functools.partial(on_device, mesh.shape["expert"], mesh.shape["token"]),
        mesh=mesh,
        in_specs=placed,
        out_specs=(P(("expert", "token"), None, None), P("expert")),
        check_vma=False,
    )
```
